256 devices in a mesh: ctx: 64 (over x, z, core), head: 4 (over y).
Axes of the slice: x: 4, y: 4, z: 8, core: 2. Of those that a mesh axis runs over, the one named last changes fastest.
Arguments:
- x_stream: bfloat16 [16384, 4096], P('ctx', 'head'), may hold values from -6 to 6
- z_stream: bfloat16 [16384, 4096], P('ctx', 'head'), may hold values from -6 to 6
- b_stream: bfloat16 [16384, 512], P('ctx', 'head'), may hold values from -6 to 6
- c_stream: bfloat16 [16384, 512], P('ctx', 'head'), may hold values from -6 to 6
- step_size: float32 [16384, 64], P('ctx', 'head'), may hold values from 0 to 3
- log_decay: float32 [16384, 64], P('ctx', 'head'), may hold values from -1 to 0
- kernel_x: bfloat16 [4, 4096], P(None, 'head'), may hold values from -3 to 3
- kernel_b: bfloat16 [4, 512], P(None, 'head'), may hold values from -3 to 3
- kernel_c: bfloat16 [4, 512], P(None, 'head'), may hold values from -3 to 3
- skip_gain: float32 [64], P('head'), may hold values from 1 to 8
- norm_gain: float32 [4096], P('head'), may hold values from 0.25 to 1.75
- out_weight: bfloat16 [4096, 4096], P('head'), may hold values from -0.125 to 0.125
Outputs:
- layer_out: bfloat16 [16384, 4096], P('ctx', 'head')
The draws below stay inside these ranges and needn't reach their ends.
All inputs are finite; a program needn't handle non-finite values.
Results may differ from the reference program's by a relative error of at most 0.013.
Values may be sent and summed in bfloat16 or wider, within the bound.
A program may use at most 128 MiB of HBM per device.

```python
import math
import jax
import jax.numpy as jnp
from jax import lax

D = 4096
HEAD_SHARE = 64
P_SIZE = 64
N = 128
GROUPS = 4
CONV = 4
SPAN = 256
TOK_DEV = 256
TOKEN_COUNT = 16384
INNER = 4096
GN = 512
N_HEAD = 4


def head_rate_draw(key):
    key_one, key_two, key_three = jax.random.split(jax.random.fold_in(key, 7), 3)
    quick_share = 0.5
    fast_head_set = jax.random.uniform(key_one, (HEAD_SHARE,)) < quick_share
    quick_rate = jnp.exp(jax.random.uniform(key_two, (HEAD_SHARE,), minval=math.log(1.0 / 50.0), maxval=math.log(1.0 / 30.0)))
    slow_rate = jnp.exp(jax.random.uniform(key_three, (HEAD_SHARE,), minval=math.log(0.1), maxval=math.log(0.35))) / TOKEN_COUNT
    return (jnp.where(fast_head_set, quick_rate, slow_rate), fast_head_set)


def draw_log_decay(key, part):
    head_frequency, fast_head_set = head_rate_draw(key)
    random_key_list = jax.random.split(jax.random.fold_in(key, 11), 4)
    block_count = TOKEN_COUNT // TOK_DEV
    device_multiplier = jnp.exp(jax.random.uniform(random_key_list[0], (block_count, HEAD_SHARE), minval=-math.log(2.0), maxval=math.log(2.0)))
    device_multiplier = jnp.repeat(device_multiplier, TOK_DEV, axis=0)
    jaggedness_level = jax.random.uniform(random_key_list[1], (TOKEN_COUNT, HEAD_SHARE), minval=0.5, maxval=1.5)
    spike_positions = jax.random.randint(random_key_list[2], (3,), 0, TOKEN_COUNT)
    spike_row_list = jnp.any(jnp.arange(TOKEN_COUNT)[:, None] == spike_positions[None, :], axis=1)
    spike_penalty = jax.random.uniform(random_key_list[3], (TOKEN_COUNT, HEAD_SHARE), minval=0.22, maxval=0.69)
    token_frequency = jnp.where(spike_row_list[:, None] & jnp.logical_not(fast_head_set)[None, :], spike_penalty, head_frequency[None, :] * device_multiplier * jaggedness_level)
    return (-token_frequency).astype(jnp.float32)


def draw_step_size(key, part):
    head_frequency, fast_head_set = head_rate_draw(key)
    rough_key = jax.random.fold_in(key, 13)
    jaggedness_level = jax.random.uniform(rough_key, (TOKEN_COUNT, HEAD_SHARE), minval=0.5, maxval=2.0)
    return (jaggedness_level * jnp.sqrt(head_frequency * 40.0)[None, :]).astype(jnp.float32)


def raised(entries, own_key, source, target, blocks, factor):
    def block_of(axis_at):
        return (jnp.arange(entries.shape[axis_at]) // (entries.shape[axis_at] // blocks)).reshape((-1,) + (1,) * (entries.ndim - 1 - axis_at))

    first = jax.random.permutation(own_key, blocks)[block_of(target)]
    second = (block_of(target) + blocks // 2) % blocks
    return jnp.where((block_of(source) == first) | (block_of(source) == second), factor * entries, entries)


def level_of(stream_key, shape, cuts, least, high):
    factor_of = 1.0
    for dim, parts in cuts:
        draws = jax.random.uniform(jax.random.fold_in(jax.random.fold_in(stream_key, 6), dim), (parts,), jnp.float32, least / len(cuts), high / len(cuts))
        factor_of = factor_of * jnp.repeat(jnp.exp(draws), shape[dim] // parts).reshape((-1,) + (1,) * (len(shape) - 1 - dim))
    return factor_of


def centred(rng, shape, spread, most, cuts=(), kind=jnp.bfloat16):
    values = jax.random.normal(rng, shape, jnp.float32) * spread
    if len(cuts) > 0:
        values = level_of(rng, shape, cuts, -0.22, 0.18) * values
    return jnp.clip(values, min=-most, max=most).astype(kind)


def heavy_noise(rng, extent, spread, most, cuts, heavy, held_as=jnp.bfloat16):
    values = spread * jax.random.normal(rng, extent, jnp.float32)
    if cuts:
        values = values * level_of(rng, extent, cuts, -0.22, 0.18)
    return jnp.clip(raised(values, jax.random.fold_in(rng, 3), *heavy), -most, most).astype(held_as)


def setup_inputs(seed: int = 0) -> dict:
    key_of = jax.random.split(jax.random.key(seed), 13)
    x_stream = centred(key_of[0], (TOKEN_COUNT, INNER), 1.0, 6.0, ((0, 64), (1, 4)))
    z_stream = centred(key_of[1], (TOKEN_COUNT, INNER), 1.0, 6.0, ((0, 64), (1, 4)))
    b_stream = centred(key_of[2], (TOKEN_COUNT, GN), 1.0, 6.0, ((0, 64), (1, 4)))
    c_stream = centred(key_of[3], (TOKEN_COUNT, GN), 1.0, 6.0, ((0, 64), (1, 4)))
    step_size = draw_step_size(jax.random.fold_in(key_of[12], 71), 0)
    log_decay = draw_log_decay(jax.random.fold_in(key_of[12], 71), 0)
    kernel_x = centred(key_of[6], (CONV, INNER), CONV ** -0.5, 3.0, ((1, 4),))
    kernel_b = centred(key_of[7], (CONV, GN), CONV ** -0.5, 3.0, ((1, 4),))
    kernel_c = centred(key_of[8], (CONV, GN), CONV ** -0.5, 3.0, ((1, 4),))
    skip_gain = jnp.clip(jnp.exp(math.log(8.0) - 2.0794415 * jax.random.uniform(key_of[9], (HEAD_SHARE,), jnp.float32) ** level_of(key_of[9], (HEAD_SHARE,), ((0, 4),), -0.2, 0.2)), 1.0, 8.0)
    norm_gain = jnp.clip(1.0 + 0.15 * jax.random.normal(key_of[10], (INNER,), jnp.float32), 0.25, 1.75)
    out_weight = heavy_noise(key_of[11], (INNER, D), INNER ** -0.5, 0.125, ((0, 4),), (0, 1, 4, 2.0))
    return dict(x_stream=x_stream, z_stream=z_stream, b_stream=b_stream, c_stream=c_stream, step_size=step_size, log_decay=log_decay, kernel_x=kernel_x, kernel_b=kernel_b, kernel_c=kernel_c, skip_gain=skip_gain, norm_gain=norm_gain, out_weight=out_weight)


def conv_silu(stream, kernel):
    length = stream.shape[0]
    padded = jnp.pad(stream.astype(jnp.float32), ((CONV - 1, 0), (0, 0)))
    running = jnp.zeros((length, stream.shape[1]), jnp.float32)
    for offset in range(CONV):
        running = running + padded[offset:offset + length] * kernel[offset].astype(jnp.float32)
    return jax.nn.silu(running).astype(jnp.bfloat16)

def span_step(carry_state, pieces):
    x_block, b_block, c_block, step_block, decay_block = pieces
    cumlog = jnp.cumsum(decay_block, axis=0)
    scores = jnp.einsum('tgn,sgn->gts', c_block.astype(jnp.float32), b_block.astype(jnp.float32))
    decay_sums = jnp.transpose(cumlog, (1, 2, 0))
    decay_gap = decay_sums[:, :, :, None] - decay_sums[:, :, None, :]
    causal = jnp.arange(SPAN)[:, None] >= jnp.arange(SPAN)[None, :]
    factor_ts = jnp.where(causal, jnp.exp(jnp.where(causal, decay_gap, 0.0)), 0.0)
    step_cols = jnp.transpose(step_block, (1, 2, 0))[:, :, None, :]
    mixing = (scores[:, None] * factor_ts * step_cols).astype(jnp.bfloat16)
    intra_out = jnp.einsum('gkts,sgkp->tgkp', mixing.astype(jnp.float32), x_block.astype(jnp.float32))
    carried = jnp.einsum('tgn,gkpn->tgkp', c_block.astype(jnp.float32), carry_state, precision=lax.Precision.HIGHEST) * jnp.exp(cumlog)[..., None]
    block_total = cumlog[-1]
    input_weight = jnp.exp(block_total[None] - cumlog) * step_block
    scaled = (x_block.astype(jnp.float32) * input_weight[..., None]).astype(jnp.bfloat16)
    new_state = jnp.exp(block_total)[..., None, None] * carry_state + jnp.einsum('tgkp,tgn->gkpn', scaled.astype(jnp.float32), b_block.astype(jnp.float32))
    return (new_state, intra_out + carried)

def reference(x_stream, z_stream, b_stream, c_stream, step_size, log_decay, kernel_x, kernel_b, kernel_c, skip_gain, norm_gain, out_weight):
    x_conv = conv_silu(x_stream, kernel_x)
    b_conv = conv_silu(b_stream, kernel_b)
    c_conv = conv_silu(c_stream, kernel_c)
    span_count = TOKEN_COUNT // SPAN
    per_group = HEAD_SHARE // GROUPS
    x_spans = x_conv.reshape(span_count, SPAN, GROUPS, per_group, P_SIZE)
    b_spans = b_conv.reshape(span_count, SPAN, GROUPS, N)
    c_spans = c_conv.reshape(span_count, SPAN, GROUPS, N)
    step_spans = step_size.reshape(span_count, SPAN, GROUPS, per_group)
    decay_spans = log_decay.reshape(span_count, SPAN, GROUPS, per_group)
    zero_state = jnp.zeros((GROUPS, per_group, P_SIZE, N), jnp.float32)
    final_state, ssd_out = lax.scan(span_step, zero_state, (x_spans, b_spans, c_spans, step_spans, decay_spans))
    ssd_out = ssd_out.reshape(TOKEN_COUNT, HEAD_SHARE, P_SIZE) + skip_gain[None, :, None] * x_conv.astype(jnp.float32).reshape(TOKEN_COUNT, HEAD_SHARE, P_SIZE)
    gated_out = ssd_out.reshape(TOKEN_COUNT, INNER) * jax.nn.silu(z_stream.astype(jnp.float32))
    grouped = gated_out.reshape(TOKEN_COUNT, GROUPS, INNER // GROUPS)
    inverse_rms = lax.rsqrt(lax.optimization_barrier(jnp.mean(grouped * grouped, axis=2, keepdims=True)) + 1e-05)
    normed = ((grouped * inverse_rms).reshape(TOKEN_COUNT, INNER) * norm_gain[None, :]).astype(jnp.bfloat16)
    block_width = INNER // N_HEAD
    token_blocks = normed.reshape(TOKEN_COUNT // TOK_DEV, TOK_DEV, INNER)

    def project(token_rows):
        running = jnp.zeros((TOK_DEV, D), jnp.float32)
        for block_index in range(N_HEAD):
            lower = block_index * block_width
            part_sum = jnp.dot(token_rows[:, lower:lower + block_width], out_weight[lower:lower + block_width], preferred_element_type=jnp.float32).astype(jnp.bfloat16)
            part_sum = lax.optimization_barrier(part_sum)
            running = running + part_sum.astype(jnp.float32)
        return running.astype(jnp.bfloat16)
    return lax.map(project, token_blocks).reshape(TOKEN_COUNT, D)
```

```python
import jax
import jax.numpy as jnp
from jax import lax
from jax.experimental import pallas as pl
from jax.experimental.pallas import tpu as pltpu
from jax.sharding import PartitionSpec as P

TOK = 256
CH = 1024
HEADS = 16
N = 128
LINE = 16
XS = 4
ROWS = N // LINE
PIECES = 4
PW = CH // PIECES
MESH = pl.DeviceIdType.MESH
F32 = jnp.float32
BF16 = jnp.bfloat16


def dot(a, b):
    return jnp.dot(a, b, preferred_element_type=F32)


def split3(v):
    hi = v.astype(BF16)
    rest = v - hi.astype(F32)
    mid = rest.astype(BF16)
    low = (rest - mid.astype(F32)).astype(BF16)
    return hi, mid, low


def dot_exact_right(v, onehot):
    hi, mid, low = split3(v)
    return dot(hi, onehot) + dot(mid, onehot) + dot(low, onehot)


def dot_exact_left(onehot, v):
    hi, mid, low = split3(v)
    return dot(onehot, hi) + dot(onehot, mid) + dot(onehot, low)


def silu(v):
    return v * (1.0 / (1.0 + jnp.exp(-v)))


def spread(rows, lanes, width):
    head = lax.broadcasted_iota(jnp.int32, (rows, lanes), 0)
    lane = lax.broadcasted_iota(jnp.int32, (rows, lanes), 1)
    return ((lane >= head * width) & (lane < head * width + width)).astype(F32).astype(BF16)


def conv_rolled(v, k):
    total = k[3:4] * v
    for shift in (1, 2, 3):
        total = total + k[3 - shift : 4 - shift] * pltpu.roll(v, shift, 0)
    return silu(total)


def conv_head(halo, v, k):
    joined = jnp.concatenate([halo[8:16].astype(F32), v[0:16].astype(F32)], axis=0)
    return conv_rolled(joined, k)[8:24]


def kernel(
    x_hbm, z_hbm, b_ref, c_ref, step_ref, decay_ref, kx_ref, kb_ref, kc_ref, skip_ref, gain_ref,
    w_hbm, o_ref,
    x_v, z_v, w_v, xc, bc, cc, halo_x, halo_b, halo_c,
    cum_t, step_t, cum_wide, in_w, gate_a, gate_b, scores, skip_wide,
    dl_send, dl_recv, dlx_send, dlx_recv,
    st_send, st_recv, excl, g_send, g_recv, pf_send, pf_recv, normed,
    diag_send, diag_recv, near_send, near_keep, near_recv, own,
    local_sem, halo_ssem, halo_rsem, dl_ssem, dl_rsem, dlx_ssem, dlx_rsem,
    st_ssem, st_rsem, g_ssem, g_rsem, pf_ssem, pf_rsem,
    diag_ssem, diag_rsem, near_ssem, near_rsem,
):
    ctx = lax.axis_index("ctx")
    y = lax.axis_index("head")
    ctx_count = LINE * XS
    xi = ctx // LINE
    pos = lax.rem(ctx, LINE)
    base = xi * LINE
    right = lax.rem(y + 1, 4)
    left = lax.rem(y + 3, 4)
    across = lax.rem(y + 2, 4)

    barrier = pltpu.get_barrier_semaphore()

    def greet_line(i, carry):
        pl.semaphore_signal(
            barrier, inc=1, device_id={"ctx": base + lax.rem(pos + i, LINE)}, device_id_type=MESH
        )
        return carry

    def greet_x(i, carry):
        pl.semaphore_signal(
            barrier, inc=1, device_id={"ctx": lax.rem(xi + i, XS) * LINE + pos}, device_id_type=MESH
        )
        return carry

    lax.fori_loop(1, LINE, greet_line, 0)
    lax.fori_loop(1, XS, greet_x, 0)
    for near in (right, left):
        pl.semaphore_signal(barrier, inc=1, device_id={"head": near}, device_id_type=MESH)
    for step in (1, ctx_count - 1):
        pl.semaphore_signal(
            barrier, inc=1, device_id={"ctx": lax.rem(ctx + step, ctx_count)}, device_id_type=MESH
        )

    load_x = pltpu.make_async_copy(x_hbm, x_v, local_sem.at[0])
    load_z = pltpu.make_async_copy(z_hbm, z_v, local_sem.at[1])
    load_w = pltpu.make_async_copy(w_hbm, w_v, local_sem.at[2])
    load_x.start()
    load_z.start()
    load_w.start()

    row = lax.broadcasted_iota(jnp.int32, (TOK, TOK), 0)
    col = lax.broadcasted_iota(jnp.int32, (TOK, TOK), 1)
    lower = (row >= col).astype(F32).astype(BF16)
    step = step_ref[...]
    cum = dot_exact_left(lower, decay_ref[...])
    last = cum[TOK - 1 : TOK, :]
    weight = jnp.exp(last - cum) * step
    cum_t[...] = cum.T
    step_t[...] = step.T
    wide = spread(HEADS, HEADS * 128, 128)
    expand = spread(HEADS, CH, 64)
    cum_wide[...] = dot_exact_right(cum, wide)
    in_w[...] = dot_exact_right(weight, expand)
    dl_send[...] = dot_exact_right(jnp.broadcast_to(last, (8, HEADS)), spread(HEADS, N, 1))[0:1]

    load_x.wait()

    def conv_block(p, carry):
        lanes = pl.ds(pl.multiple_of(p * 128, 128), 128)
        xc[:, lanes] = conv_rolled(x_v[:, lanes].astype(F32), kx_ref[:, lanes].astype(F32)).astype(BF16)
        return carry

    lax.fori_loop(0, CH // 128, conv_block, 0)
    bc[...] = conv_rolled(b_ref[...].astype(F32), kb_ref[...].astype(F32)).astype(BF16)
    cc[...] = conv_rolled(c_ref[...].astype(F32), kc_ref[...].astype(F32)).astype(BF16)

    pl.semaphore_wait(barrier, LINE - 1 + XS - 1 + 2 + 2)

    def halo_copies():
        parts = ((x_v, halo_x), (b_ref, halo_b), (c_ref, halo_c))
        return [
            pltpu.make_async_remote_copy(
                src_ref=src.at[pl.ds(TOK - 16, 16)],
                dst_ref=dst,
                send_sem=halo_ssem.at[i],
                recv_sem=halo_rsem.at[i],
                device_id={"ctx": lax.rem(ctx + 1, ctx_count)},
                device_id_type=MESH,
            )
            for i, (src, dst) in enumerate(parts)
        ]

    for copy in halo_copies():
        copy.start()

    def dl_copy(i, slot):
        to = lax.rem(pos + i, LINE)
        return pltpu.make_async_remote_copy(
            src_ref=dl_send,
            dst_ref=dl_recv.at[slot],
            send_sem=dl_ssem.at[i],
            recv_sem=dl_rsem.at[slot],
            device_id={"ctx": base + to},
            device_id_type=MESH,
        )

    def st_copy(i, slot):
        to = lax.rem(pos + i, LINE)
        return pltpu.make_async_remote_copy(
            src_ref=st_send.at[to],
            dst_ref=st_recv.at[slot],
            send_sem=st_ssem.at[i],
            recv_sem=st_rsem.at[slot],
            device_id={"ctx": base + to},
            device_id_type=MESH,
        )

    def pf_copy(i, slot):
        to = lax.rem(pos + i, LINE)
        return pltpu.make_async_remote_copy(
            src_ref=pf_send.at[to],
            dst_ref=pf_recv.at[slot],
            send_sem=pf_ssem.at[i],
            recv_sem=pf_rsem.at[slot],
            device_id={"ctx": base + to},
            device_id_type=MESH,
        )

    def dlx_copy(i, slot):
        return pltpu.make_async_remote_copy(
            src_ref=dlx_send,
            dst_ref=dlx_recv.at[slot],
            send_sem=dlx_ssem.at[i],
            recv_sem=dlx_rsem.at[slot],
            device_id={"ctx": lax.rem(xi + i, XS) * LINE + pos},
            device_id_type=MESH,
        )

    def g_copy(i, slot):
        return pltpu.make_async_remote_copy(
            src_ref=g_send,
            dst_ref=g_recv.at[slot],
            send_sem=g_ssem.at[i],
            recv_sem=g_rsem.at[slot],
            device_id={"ctx": lax.rem(xi + i, XS) * LINE + pos},
            device_id_type=MESH,
        )

    def start_all(make, count, here):
        def one(i, carry):
            make(i, here).start()
            return carry

        lax.fori_loop(1, count, one, 0)

    def wait_all(make, count, here):
        def one(i, carry):
            copy = make(i, lax.rem(here + i, count))
            copy.wait_send()
            copy.wait_recv()
            return carry

        lax.fori_loop(1, count, one, 0)

    start_all(dl_copy, LINE, pos)

    for copy in halo_copies():
        copy.wait()

    first = ctx == 0

    def halo_value(ref):
        v = ref[...].astype(F32)
        return jnp.where(first, jnp.zeros_like(v), v)

    xc[0:16, :] = conv_head(halo_value(halo_x), x_v[0:16, :], kx_ref[...].astype(F32)).astype(BF16)
    bc[0:16, :] = conv_head(halo_value(halo_b), b_ref[0:16, :], kb_ref[...].astype(F32)).astype(BF16)
    cc[0:16, :] = conv_head(halo_value(halo_c), c_ref[0:16, :], kc_ref[...].astype(F32)).astype(BF16)

    b_cols = bc[...].astype(F32).T.astype(BF16)

    def state_block(p, carry):
        lanes = pl.ds(pl.multiple_of(p * 128, 128), 128)
        scaled = (xc[:, lanes].astype(F32) * in_w[:, lanes]).astype(BF16)
        st_send[:, :, lanes] = dot(b_cols, scaled).reshape(LINE, ROWS, 128).astype(BF16)
        return carry

    lax.fori_loop(0, CH // 128, state_block, 0)
    st_recv[pos] = st_send[pos]
    start_all(st_copy, LINE, pos)

    dl_recv[pos] = dl_send[...]
    wait_all(dl_copy, LINE, pos)
    line_decay = dl_recv[:, 0, :]
    dlx_send[...] = jnp.sum(line_decay, axis=0, keepdims=True)
    dlx_recv[xi] = dlx_send[...]
    start_all(dlx_copy, XS, xi)

    scores[...] = dot(cc[...], b_cols)
    in_w[...] = dot_exact_right(jnp.exp(cum), expand)
    skip_row = dot_exact_right(jnp.broadcast_to(skip_ref[...], (8, HEADS)), expand)[0:1]
    skip_wide[...] = skip_row
    load_z.wait()
    trow = lax.broadcasted_iota(jnp.int32, (128, 128), 0)
    tcol = lax.broadcasted_iota(jnp.int32, (128, 128), 1)
    causal = trow >= tcol

    def span_block(p, carry):
        lanes = pl.ds(pl.multiple_of(p * 128, 128), 128)
        x_pair = xc[:, lanes]
        tops, bottoms = [], []
        for e in range(2):
            h = 2 * p + e
            cols = cum_wide[:, pl.ds(pl.multiple_of(h * 128, 128), 128)]
            cum_row = cum_t[pl.ds(h, 1), :]
            step_row = step_t[pl.ds(h, 1), :]

            def mix(t, s, masked):
                gap = cols[t : t + 128] - cum_row[:, s : s + 128]
                if masked:
                    gap = jnp.where(causal, gap, -1e30)
                m = scores[t : t + 128, s : s + 128] * jnp.exp(gap) * step_row[:, s : s + 128]
                return m.astype(BF16)

            tops.append(dot(mix(0, 0, True), x_pair[0:128]))
            bottoms.append(
                dot(mix(128, 0, False), x_pair[0:128]) + dot(mix(128, 128, True), x_pair[128:256])
            )
        low = tcol < 64
        inner = jnp.concatenate(
            [jnp.where(low, tops[0], tops[1]), jnp.where(low, bottoms[0], bottoms[1])], axis=0
        )
        gate = silu(z_v[:, lanes].astype(F32))
        gate_a[:, lanes] = (inner + skip_wide[:, lanes] * x_pair.astype(F32)) * gate
        gate_b[:, lanes] = in_w[:, lanes] * gate
        return carry

    lax.fori_loop(0, CH // 128, span_block, 0)

    expand_n = spread(N, CH, 64)
    line_factor = jnp.exp(dot_exact_right(line_decay, expand_n))
    wait_all(st_copy, LINE, pos)
    running = jnp.zeros((ROWS, CH), F32)
    for j in range(LINE):
        excl[j] = running
        running = line_factor[j : j + 1] * running + st_recv[j].astype(F32)
    g_send[...] = running
    start_all(g_copy, XS, xi)

    wait_all(dlx_copy, XS, xi)
    x_decay = dlx_recv[:, 0, :]
    x_factor = jnp.exp(
        dot_exact_right(jnp.concatenate([x_decay, x_decay], axis=0), expand_n)
    )
    wait_all(g_copy, XS, xi)
    before = jnp.zeros((ROWS, CH), F32)
    for i in range(XS - 1):
        before = jnp.where(i < xi, x_factor[i : i + 1] * before + g_recv[i], before)
    for j in range(LINE):
        pf_send[j] = (excl[j] + before).astype(BF16)
        before = line_factor[j : j + 1] * before
    pf_recv[pos] = pf_send[pos]
    start_all(pf_copy, LINE, pos)
    wait_all(pf_copy, LINE, pos)

    state = pf_recv[...].astype(F32).reshape(N, CH).astype(BF16)
    c_all = cc[...]
    squares = jnp.zeros((TOK, 128), F32)
    for p in range(CH // 256):
        lanes = slice(p * 256, p * 256 + 256)
        gated = gate_a[:, lanes] + dot(c_all, state[:, lanes]) * gate_b[:, lanes]
        gate_a[:, lanes] = gated
        sq = gated * gated
        squares = squares + sq[:, 0:128] + sq[:, 128:256]
    scale = lax.rsqrt(jnp.sum(squares, axis=1, keepdims=True) * (1.0 / CH) + 1e-05)
    for p in range(CH // 256):
        lanes = slice(p * 256, p * 256 + 256)
        normed[:, lanes] = (gate_a[:, lanes] * scale * gain_ref[:, lanes]).astype(BF16)

    load_w.wait()

    def product(owner, j):
        lanes = pl.ds(pl.multiple_of(owner * CH + j * PW, PW), PW)
        return dot(normed[...], w_v[:, lanes])

    sides = (right, left)
    diag_rows = (0, 128)
    near_rows = (128, 0)

    def diag_copy(side, j):
        return pltpu.make_async_remote_copy(
            src_ref=diag_send.at[side, j],
            dst_ref=diag_recv.at[side, j],
            send_sem=diag_ssem.at[side, j],
            recv_sem=diag_rsem.at[side, j],
            device_id={"head": sides[side]},
            device_id_type=MESH,
        )

    def near_copy(side, relayed, j):
        return pltpu.make_async_remote_copy(
            src_ref=near_send.at[side, relayed, j],
            dst_ref=near_recv.at[side, relayed, j],
            send_sem=near_ssem.at[side, relayed, j],
            recv_sem=near_rsem.at[side, relayed, j],
            device_id={"head": sides[side]},
            device_id_type=MESH,
        )

    def across_step(j, carry):
        part = product(across, j).astype(BF16)
        for side in range(2):
            diag_send[side, j] = part[diag_rows[side] : diag_rows[side] + 128]
            diag_copy(side, j).start()
        return carry

    lax.fori_loop(0, PIECES, across_step, 0)

    def near_step(j, carry):
        for side in range(2):
            part = product(sides[side], j).astype(BF16)
            near_send[side, 0, j] = part[near_rows[side] : near_rows[side] + 128]
            near_copy(side, 0, j).start()
            near_keep[side, j] = part[diag_rows[side] : diag_rows[side] + 128]
        return carry

    lax.fori_loop(0, PIECES, near_step, 0)

    def relay_step(j, carry):
        for side in range(2):
            diag_copy(side, j).wait()
            total = near_keep[side, j].astype(F32) + diag_recv[side, j].astype(F32)
            near_send[side, 1, j] = total.astype(BF16)
            near_copy(side, 1, j).start()
        return carry

    lax.fori_loop(0, PIECES, relay_step, 0)

    def own_step(j, carry):
        own[j] = product(y, j)
        return carry

    lax.fori_loop(0, PIECES, own_step, 0)

    for relayed in range(2):
        def last_step(j, carry):
            for side in range(2):
                near_copy(side, relayed, j).wait()
            return carry

        lax.fori_loop(0, PIECES, last_step, 0)
    for j in range(PIECES):
        lanes = slice(j * PW, j * PW + PW)
        mine = own[j].astype(BF16).astype(F32)
        top = near_recv[0, 1, j].astype(F32) + near_recv[1, 0, j].astype(F32)
        bottom = near_recv[0, 0, j].astype(F32) + near_recv[1, 1, j].astype(F32)
        o_ref[0:128, lanes] = (mine[0:128] + top).astype(BF16)
        o_ref[128:256, lanes] = (mine[128:256] + bottom).astype(BF16)


def body(x, z, b, c, step, decay, kx, kb, kc, skip, gain, w):
    vm = pl.BlockSpec(memory_space=pltpu.VMEM)
    hbm = pl.BlockSpec(memory_space=pl.ANY)
    dma = pltpu.SemaphoreType.DMA
    return pl.pallas_call(
        kernel,
        out_shape=jax.ShapeDtypeStruct((TOK, CH), BF16),
        in_specs=[hbm, hbm] + [vm] * 9 + [hbm],
        out_specs=vm,
        scratch_shapes=[
            pltpu.VMEM((TOK, CH), BF16),
            pltpu.VMEM((TOK, CH), BF16),
            pltpu.VMEM((CH, 4 * CH), BF16),
            pltpu.VMEM((TOK, CH), BF16),
            pltpu.VMEM((TOK, N), BF16),
            pltpu.VMEM((TOK, N), BF16),
            pltpu.VMEM((16, CH), BF16),
            pltpu.VMEM((16, N), BF16),
            pltpu.VMEM((16, N), BF16),
            pltpu.VMEM((HEADS, TOK), F32),
            pltpu.VMEM((HEADS, TOK), F32),
            pltpu.VMEM((TOK, HEADS * 128), F32),
            pltpu.VMEM((TOK, CH), F32),
            pltpu.VMEM((TOK, CH), F32),
            pltpu.VMEM((TOK, CH), F32),
            pltpu.VMEM((TOK, TOK), F32),
            pltpu.VMEM((1, CH), F32),
            pltpu.VMEM((1, N), F32),
            pltpu.VMEM((LINE, 1, N), F32),
            pltpu.VMEM((1, N), F32),
            pltpu.VMEM((XS, 1, N), F32),
            pltpu.VMEM((LINE, ROWS, CH), BF16),
            pltpu.VMEM((LINE, ROWS, CH), BF16),
            pltpu.VMEM((LINE, ROWS, CH), F32),
            pltpu.VMEM((ROWS, CH), F32),
            pltpu.VMEM((XS, ROWS, CH), F32),
            pltpu.VMEM((LINE, ROWS, CH), BF16),
            pltpu.VMEM((LINE, ROWS, CH), BF16),
            pltpu.VMEM((TOK, CH), BF16),
            pltpu.VMEM((2, PIECES, 128, PW), BF16),
            pltpu.VMEM((2, PIECES, 128, PW), BF16),
            pltpu.VMEM((2, 2, PIECES, 128, PW), BF16),
            pltpu.VMEM((2, PIECES, 128, PW), BF16),
            pltpu.VMEM((2, 2, PIECES, 128, PW), BF16),
            pltpu.VMEM((PIECES, TOK, PW), F32),
            dma((3,)),
            dma((3,)),
            dma((3,)),
            dma((LINE,)),
            dma((LINE,)),
            dma((XS,)),
            dma((XS,)),
            dma((LINE,)),
            dma((LINE,)),
            dma((XS,)),
            dma((XS,)),
            dma((LINE,)),
            dma((LINE,)),
            dma((2, PIECES)),
            dma((2, PIECES)),
            dma((2, 2, PIECES)),
            dma((2, 2, PIECES)),
        ],
        compiler_params=pltpu.CompilerParams(collective_id=0, has_side_effects=True),
        name="ssm_layer",
    )(x, z, b, c, step, decay, kx, kb, kc, skip.reshape(1, HEADS), gain.reshape(1, CH), w)


def solution(mesh):
    placed = (
        P("ctx", "head"),
        P("ctx", "head"),
        P("ctx", "head"),
        P("ctx", "head"),
        P("ctx", "head"),
        P("ctx", "head"),
        P(None, "head"),
        P(None, "head"),
        P(None, "head"),
        P("head"),
        P("head"),
        P("head", None),
    )
    return jax.shard_map(
        body, mesh=mesh, in_specs=placed, out_specs=P("ctx", "head"), check_vma=False
    )
```

```python
import jax
import jax.numpy as jnp
from jax import lax
from jax.experimental import pallas as pl
from jax.experimental.pallas import tpu as pltpu
from jax.sharding import PartitionSpec as P

TOK = 256
CH = 1024
HEADS = 16
N = 128
LINE = 16
XS = 4
ROWS = N // LINE
PIECES = 4
PW = CH // PIECES
MESH = pl.DeviceIdType.MESH
F32 = jnp.float32
BF16 = jnp.bfloat16


def dot(a, b):
    return jnp.dot(a, b, preferred_element_type=F32)


def split3(v):
    hi = v.astype(BF16)
    rest = v - hi.astype(F32)
    mid = rest.astype(BF16)
    low = (rest - mid.astype(F32)).astype(BF16)
    return hi, mid, low


def dot_exact_right(v, onehot):
    hi, mid, low = split3(v)
    return dot(hi, onehot) + dot(mid, onehot) + dot(low, onehot)


def dot_exact_left(onehot, v):
    hi, mid, low = split3(v)
    return dot(onehot, hi) + dot(onehot, mid) + dot(onehot, low)


def silu(v):
    return v * (1.0 / (1.0 + jnp.exp(-v)))


def spread(rows, lanes, width):
    head = lax.broadcasted_iota(jnp.int32, (rows, lanes), 0)
    lane = lax.broadcasted_iota(jnp.int32, (rows, lanes), 1)
    return ((lane >= head * width) & (lane < head * width + width)).astype(F32).astype(BF16)


def conv_rolled(v, k):
    total = k[3:4] * v
    for shift in (1, 2, 3):
        total = total + k[3 - shift : 4 - shift] * pltpu.roll(v, shift, 0)
    return silu(total)


def conv_head(halo, v, k):
    joined = jnp.concatenate([halo[8:16].astype(F32), v[0:16].astype(F32)], axis=0)
    return conv_rolled(joined, k)[8:24]


def kernel(
    x_hbm, z_hbm, b_ref, c_ref, step_t, decay_t, kx_ref, kb_ref, kc_ref, skip_ref, gain_ref,
    w_hbm, o_ref,
    x_v, z_v, w_v, xc, bc, cc, halo_x, halo_b, halo_c,
    cum_t, cum_wide, in_w, gate_a, gate_b, scores, skip_wide,
    dl_send, dl_recv, dlx_send, dlx_recv,
    st_send, st_recv, excl, g_send, g_recv, pf_send, pf_recv, normed,
    diag_send, diag_recv, near_send, near_keep, near_recv, own,
    local_sem, halo_ssem, halo_rsem, dl_ssem, dl_rsem, dlx_ssem, dlx_rsem,
    st_ssem, st_rsem, g_ssem, g_rsem, pf_ssem, pf_rsem,
    diag_ssem, diag_rsem, near_ssem, near_rsem,
):
    ctx = lax.axis_index("ctx")
    y = lax.axis_index("head")
    ctx_count = LINE * XS
    xi = ctx // LINE
    pos = lax.rem(ctx, LINE)
    base = xi * LINE
    right = lax.rem(y + 1, 4)
    left = lax.rem(y + 3, 4)
    across = lax.rem(y + 2, 4)

    barrier = pltpu.get_barrier_semaphore()

    def greet_line(i, carry):
        pl.semaphore_signal(
            barrier, inc=1, device_id={"ctx": base + lax.rem(pos + i, LINE)}, device_id_type=MESH
        )
        return carry

    def greet_x(i, carry):
        pl.semaphore_signal(
            barrier, inc=1, device_id={"ctx": lax.rem(xi + i, XS) * LINE + pos}, device_id_type=MESH
        )
        return carry

    lax.fori_loop(1, LINE, greet_line, 0)
    lax.fori_loop(1, XS, greet_x, 0)
    for near in (right, left):
        pl.semaphore_signal(barrier, inc=1, device_id={"head": near}, device_id_type=MESH)
    for step in (1, ctx_count - 1):
        pl.semaphore_signal(
            barrier, inc=1, device_id={"ctx": lax.rem(ctx + step, ctx_count)}, device_id_type=MESH
        )

    load_x = pltpu.make_async_copy(x_hbm, x_v, local_sem.at[0])
    load_z = pltpu.make_async_copy(z_hbm, z_v, local_sem.at[1])
    load_w = pltpu.make_async_copy(w_hbm, w_v, local_sem.at[2])
    load_x.start()
    load_z.start()
    load_w.start()

    row = lax.broadcasted_iota(jnp.int32, (TOK, TOK), 0)
    col = lax.broadcasted_iota(jnp.int32, (TOK, TOK), 1)
    upper = (row <= col).astype(F32).astype(BF16)
    sums = dot_exact_right(decay_t[...], upper)
    cum_t[...] = sums
    cum = sums.T
    last = cum[TOK - 1 : TOK, :]
    weight = (jnp.exp(sums[:, TOK - 1 : TOK] - sums) * step_t[...]).T
    wide = spread(HEADS, HEADS * 128, 128)
    expand = spread(HEADS, CH, 64)
    cum_wide[...] = dot_exact_right(cum, wide)
    in_w[...] = dot_exact_right(weight, expand)
    dl_send[...] = dot_exact_right(jnp.broadcast_to(last, (8, HEADS)), spread(HEADS, N, 1))[0:1]

    load_x.wait()

    def conv_block(p, carry):
        lanes = pl.ds(pl.multiple_of(p * 128, 128), 128)
        xc[:, lanes] = conv_rolled(x_v[:, lanes].astype(F32), kx_ref[:, lanes].astype(F32)).astype(BF16)
        return carry

    lax.fori_loop(0, CH // 128, conv_block, 0)
    bc[...] = conv_rolled(b_ref[...].astype(F32), kb_ref[...].astype(F32)).astype(BF16)
    cc[...] = conv_rolled(c_ref[...].astype(F32), kc_ref[...].astype(F32)).astype(BF16)

    pl.semaphore_wait(barrier, LINE - 1 + XS - 1 + 2 + 2)

    def halo_copies():
        parts = ((x_v, halo_x), (b_ref, halo_b), (c_ref, halo_c))
        return [
            pltpu.make_async_remote_copy(
                src_ref=src.at[pl.ds(TOK - 16, 16)],
                dst_ref=dst,
                send_sem=halo_ssem.at[i],
                recv_sem=halo_rsem.at[i],
                device_id={"ctx": lax.rem(ctx + 1, ctx_count)},
                device_id_type=MESH,
            )
            for i, (src, dst) in enumerate(parts)
        ]

    for copy in halo_copies():
        copy.start()

    def dl_copy(i, slot):
        to = lax.rem(pos + i, LINE)
        return pltpu.make_async_remote_copy(
            src_ref=dl_send,
            dst_ref=dl_recv.at[slot],
            send_sem=dl_ssem.at[i],
            recv_sem=dl_rsem.at[slot],
            device_id={"ctx": base + to},
            device_id_type=MESH,
        )

    def st_copy(i, slot):
        to = lax.rem(pos + i, LINE)
        return pltpu.make_async_remote_copy(
            src_ref=st_send.at[to],
            dst_ref=st_recv.at[slot],
            send_sem=st_ssem.at[i],
            recv_sem=st_rsem.at[slot],
            device_id={"ctx": base + to},
            device_id_type=MESH,
        )

    def pf_copy(i, slot):
        to = lax.rem(pos + i, LINE)
        return pltpu.make_async_remote_copy(
            src_ref=pf_send.at[to],
            dst_ref=pf_recv.at[slot],
            send_sem=pf_ssem.at[i],
            recv_sem=pf_rsem.at[slot],
            device_id={"ctx": base + to},
            device_id_type=MESH,
        )

    def dlx_copy(i, slot):
        return pltpu.make_async_remote_copy(
            src_ref=dlx_send,
            dst_ref=dlx_recv.at[slot],
            send_sem=dlx_ssem.at[i],
            recv_sem=dlx_rsem.at[slot],
            device_id={"ctx": lax.rem(xi + i, XS) * LINE + pos},
            device_id_type=MESH,
        )

    def g_copy(i, slot):
        return pltpu.make_async_remote_copy(
            src_ref=g_send,
            dst_ref=g_recv.at[slot],
            send_sem=g_ssem.at[i],
            recv_sem=g_rsem.at[slot],
            device_id={"ctx": lax.rem(xi + i, XS) * LINE + pos},
            device_id_type=MESH,
        )

    def start_later(make):
        for i in range(1, XS):
            @pl.when(xi + i < XS)
            def _(i=i):
                make(i, xi).start()

    def wait_earlier(make):
        for i in range(1, XS):
            @pl.when(xi + i < XS)
            def _(i=i):
                make(i, xi).wait_send()

            @pl.when(xi >= i)
            def _(i=i):
                make(i, xi - i).wait_recv()

    def start_all(make, count, here):
        def one(i, carry):
            make(i, here).start()
            return carry

        lax.fori_loop(1, count, one, 0)

    def wait_all(make, count, here):
        def one(i, carry):
            copy = make(i, lax.rem(here + i, count))
            copy.wait_send()
            copy.wait_recv()
            return carry

        lax.fori_loop(1, count, one, 0)

    start_all(dl_copy, LINE, pos)

    for copy in halo_copies():
        copy.wait()

    first = ctx == 0

    def halo_value(ref):
        v = ref[...].astype(F32)
        return jnp.where(first, jnp.zeros_like(v), v)

    xc[0:16, :] = conv_head(halo_value(halo_x), x_v[0:16, :], kx_ref[...].astype(F32)).astype(BF16)
    bc[0:16, :] = conv_head(halo_value(halo_b), b_ref[0:16, :], kb_ref[...].astype(F32)).astype(BF16)
    cc[0:16, :] = conv_head(halo_value(halo_c), c_ref[0:16, :], kc_ref[...].astype(F32)).astype(BF16)

    b_cols = bc[...].astype(F32).T.astype(BF16)

    def state_block(p, carry):
        lanes = pl.ds(pl.multiple_of(p * 128, 128), 128)
        scaled = (xc[:, lanes].astype(F32) * in_w[:, lanes]).astype(BF16)
        st_send[:, :, lanes] = dot(b_cols, scaled).reshape(LINE, ROWS, 128).astype(BF16)
        return carry

    lax.fori_loop(0, CH // 128, state_block, 0)
    st_recv[pos] = st_send[pos]
    start_all(st_copy, LINE, pos)

    dl_recv[pos] = dl_send[...]
    wait_all(dl_copy, LINE, pos)
    line_decay = dl_recv[:, 0, :]
    dlx_send[...] = jnp.sum(line_decay, axis=0, keepdims=True)
    dlx_recv[xi] = dlx_send[...]
    start_all(dlx_copy, XS, xi)

    scores[...] = dot(cc[...], b_cols)
    in_w[...] = dot_exact_right(jnp.exp(cum), expand)
    skip_row = dot_exact_right(jnp.broadcast_to(skip_ref[...], (8, HEADS)), expand)[0:1]
    skip_wide[...] = skip_row
    load_z.wait()
    trow = lax.broadcasted_iota(jnp.int32, (128, 128), 0)
    tcol = lax.broadcasted_iota(jnp.int32, (128, 128), 1)
    causal = trow >= tcol

    def span_block(p, carry):
        lanes = pl.ds(pl.multiple_of(p * 128, 128), 128)
        x_pair = xc[:, lanes]
        tops, bottoms = [], []
        for e in range(2):
            h = 2 * p + e
            cols = cum_wide[:, pl.ds(pl.multiple_of(h * 128, 128), 128)]
            cum_row = cum_t[pl.ds(h, 1), :]
            step_row = step_t[pl.ds(h, 1), :]

            def mix(t, s, masked):
                gap = cols[t : t + 128] - cum_row[:, s : s + 128]
                if masked:
                    gap = jnp.where(causal, gap, -1e30)
                m = scores[t : t + 128, s : s + 128] * jnp.exp(gap) * step_row[:, s : s + 128]
                return m.astype(BF16)

            tops.append(dot(mix(0, 0, True), x_pair[0:128]))
            bottoms.append(
                dot(mix(128, 0, False), x_pair[0:128]) + dot(mix(128, 128, True), x_pair[128:256])
            )
        low = tcol < 64
        inner = jnp.concatenate(
            [jnp.where(low, tops[0], tops[1]), jnp.where(low, bottoms[0], bottoms[1])], axis=0
        )
        gate = silu(z_v[:, lanes].astype(F32))
        gate_a[:, lanes] = (inner + skip_wide[:, lanes] * x_pair.astype(F32)) * gate
        gate_b[:, lanes] = in_w[:, lanes] * gate
        return carry

    lax.fori_loop(0, CH // 128, span_block, 0)

    expand_n = spread(N, CH, 64)
    line_factor = jnp.exp(dot_exact_right(line_decay, expand_n))
    wait_all(st_copy, LINE, pos)
    running = jnp.zeros((ROWS, CH), F32)
    for j in range(LINE):
        excl[j] = running
        running = line_factor[j : j + 1] * running + st_recv[j].astype(F32)
    g_send[...] = running
    start_later(g_copy)

    wait_all(dlx_copy, XS, xi)
    x_decay = dlx_recv[:, 0, :]
    x_factor = jnp.exp(
        dot_exact_right(jnp.concatenate([x_decay, x_decay], axis=0), expand_n)
    )
    wait_earlier(g_copy)
    before = jnp.zeros((ROWS, CH), F32)
    for i in range(XS - 1):
        before = jnp.where(i < xi, x_factor[i : i + 1] * before + g_recv[i], before)
    for j in range(LINE):
        pf_send[j] = (excl[j] + before).astype(BF16)
        before = line_factor[j : j + 1] * before
    pf_recv[pos] = pf_send[pos]
    start_all(pf_copy, LINE, pos)
    wait_all(pf_copy, LINE, pos)

    state = pf_recv[...].astype(F32).reshape(N, CH).astype(BF16)
    c_all = cc[...]
    squares = jnp.zeros((TOK, 128), F32)
    for p in range(CH // 256):
        lanes = slice(p * 256, p * 256 + 256)
        gated = gate_a[:, lanes] + dot(c_all, state[:, lanes]) * gate_b[:, lanes]
        gate_a[:, lanes] = gated
        sq = gated * gated
        squares = squares + sq[:, 0:128] + sq[:, 128:256]
    scale = lax.rsqrt(jnp.sum(squares, axis=1, keepdims=True) * (1.0 / CH) + 1e-05)
    for p in range(CH // 256):
        lanes = slice(p * 256, p * 256 + 256)
        normed[:, lanes] = (gate_a[:, lanes] * scale * gain_ref[:, lanes]).astype(BF16)

    load_w.wait()

    def product(owner, j):
        lanes = pl.ds(pl.multiple_of(owner * CH + j * PW, PW), PW)
        return dot(normed[...], w_v[:, lanes])

    sides = (right, left)
    diag_rows = (0, 128)
    near_rows = (128, 0)

    def diag_copy(side, j):
        return pltpu.make_async_remote_copy(
            src_ref=diag_send.at[side, j],
            dst_ref=diag_recv.at[side, j],
            send_sem=diag_ssem.at[side, j],
            recv_sem=diag_rsem.at[side, j],
            device_id={"head": sides[side]},
            device_id_type=MESH,
        )

    def near_copy(side, relayed, j):
        return pltpu.make_async_remote_copy(
            src_ref=near_send.at[side, relayed, j],
            dst_ref=near_recv.at[side, relayed, j],
            send_sem=near_ssem.at[side, relayed, j],
            recv_sem=near_rsem.at[side, relayed, j],
            device_id={"head": sides[side]},
            device_id_type=MESH,
        )

    def across_step(j, carry):
        part = product(across, j).astype(BF16)
        for side in range(2):
            diag_send[side, j] = part[diag_rows[side] : diag_rows[side] + 128]
            diag_copy(side, j).start()
        return carry

    lax.fori_loop(0, PIECES, across_step, 0)

    def near_step(j, carry):
        for side in range(2):
            part = product(sides[side], j).astype(BF16)
            near_send[side, 0, j] = part[near_rows[side] : near_rows[side] + 128]
            near_copy(side, 0, j).start()
            near_keep[side, j] = part[diag_rows[side] : diag_rows[side] + 128]
        return carry

    lax.fori_loop(0, PIECES, near_step, 0)

    def relay_step(j, carry):
        for side in range(2):
            diag_copy(side, j).wait()
            total = near_keep[side, j].astype(F32) + diag_recv[side, j].astype(F32)
            near_send[side, 1, j] = total.astype(BF16)
            near_copy(side, 1, j).start()
        return carry

    lax.fori_loop(0, PIECES, relay_step, 0)

    def own_step(j, carry):
        own[j] = product(y, j)
        return carry

    lax.fori_loop(0, PIECES, own_step, 0)

    for relayed in range(2):
        def last_step(j, carry):
            for side in range(2):
                near_copy(side, relayed, j).wait()
            return carry

        lax.fori_loop(0, PIECES, last_step, 0)
    for j in range(PIECES):
        lanes = slice(j * PW, j * PW + PW)
        mine = own[j].astype(BF16).astype(F32)
        top = near_recv[0, 1, j].astype(F32) + near_recv[1, 0, j].astype(F32)
        bottom = near_recv[0, 0, j].astype(F32) + near_recv[1, 1, j].astype(F32)
        o_ref[0:128, lanes] = (mine[0:128] + top).astype(BF16)
        o_ref[128:256, lanes] = (mine[128:256] + bottom).astype(BF16)


def body(x, z, b, c, step, decay, kx, kb, kc, skip, gain, w):
    vm = pl.BlockSpec(memory_space=pltpu.VMEM)
    hbm = pl.BlockSpec(memory_space=pl.ANY)
    dma = pltpu.SemaphoreType.DMA
    return pl.pallas_call(
        kernel,
        out_shape=jax.ShapeDtypeStruct((TOK, CH), BF16),
        in_specs=[hbm, hbm] + [vm] * 9 + [hbm],
        out_specs=vm,
        scratch_shapes=[
            pltpu.VMEM((TOK, CH), BF16),
            pltpu.VMEM((TOK, CH), BF16),
            pltpu.VMEM((CH, 4 * CH), BF16),
            pltpu.VMEM((TOK, CH), BF16),
            pltpu.VMEM((TOK, N), BF16),
            pltpu.VMEM((TOK, N), BF16),
            pltpu.VMEM((16, CH), BF16),
            pltpu.VMEM((16, N), BF16),
            pltpu.VMEM((16, N), BF16),
            pltpu.VMEM((HEADS, TOK), F32),
            pltpu.VMEM((TOK, HEADS * 128), F32),
            pltpu.VMEM((TOK, CH), F32),
            pltpu.VMEM((TOK, CH), F32),
            pltpu.VMEM((TOK, CH), F32),
            pltpu.VMEM((TOK, TOK), F32),
            pltpu.VMEM((1, CH), F32),
            pltpu.VMEM((1, N), F32),
            pltpu.VMEM((LINE, 1, N), F32),
            pltpu.VMEM((1, N), F32),
            pltpu.VMEM((XS, 1, N), F32),
            pltpu.VMEM((LINE, ROWS, CH), BF16),
            pltpu.VMEM((LINE, ROWS, CH), BF16),
            pltpu.VMEM((LINE, ROWS, CH), F32),
            pltpu.VMEM((ROWS, CH), F32),
            pltpu.VMEM((XS, ROWS, CH), F32),
            pltpu.VMEM((LINE, ROWS, CH), BF16),
            pltpu.VMEM((LINE, ROWS, CH), BF16),
            pltpu.VMEM((TOK, CH), BF16),
            pltpu.VMEM((2, PIECES, 128, PW), BF16),
            pltpu.VMEM((2, PIECES, 128, PW), BF16),
            pltpu.VMEM((2, 2, PIECES, 128, PW), BF16),
            pltpu.VMEM((2, PIECES, 128, PW), BF16),
            pltpu.VMEM((2, 2, PIECES, 128, PW), BF16),
            pltpu.VMEM((PIECES, TOK, PW), F32),
            dma((3,)),
            dma((3,)),
            dma((3,)),
            dma((LINE,)),
            dma((LINE,)),
            dma((XS,)),
            dma((XS,)),
            dma((LINE,)),
            dma((LINE,)),
            dma((XS,)),
            dma((XS,)),
            dma((LINE,)),
            dma((LINE,)),
            dma((2, PIECES)),
            dma((2, PIECES)),
            dma((2, 2, PIECES)),
            dma((2, 2, PIECES)),
        ],
        compiler_params=pltpu.CompilerParams(collective_id=0, has_side_effects=True),
        name="ssm_layer",
    )(x, z, b, c, step.T, decay.T, kx, kb, kc, skip.reshape(1, HEADS), gain.reshape(1, CH), w)


def solution(mesh):
    placed = (
        P("ctx", "head"),
        P("ctx", "head"),
        P("ctx", "head"),
        P("ctx", "head"),
        P("ctx", "head"),
        P("ctx", "head"),
        P(None, "head"),
        P(None, "head"),
        P(None, "head"),
        P("head"),
        P("head"),
        P("head", None),
    )
    return jax.shard_map(
        body, mesh=mesh, in_specs=placed, out_specs=P("ctx", "head"), check_vma=False
    )
```

```python
import jax
import jax.numpy as jnp
from jax import lax
from jax.experimental import pallas as pl
from jax.experimental.pallas import tpu as pltpu
from jax.sharding import PartitionSpec as P

TOK = 256
CH = 1024
HEADS = 16
N = 128
LINE = 16
XS = 4
ROWS = N // LINE
PIECES = 4
EARLY = 3
PW = CH // PIECES
MESH = pl.DeviceIdType.MESH
F32 = jnp.float32
BF16 = jnp.bfloat16


def dot(a, b):
    return jnp.dot(a, b, preferred_element_type=F32)


def split3(v):
    hi = v.astype(BF16)
    rest = v - hi.astype(F32)
    mid = rest.astype(BF16)
    low = (rest - mid.astype(F32)).astype(BF16)
    return hi, mid, low


def dot_exact_right(v, onehot):
    hi, mid, low = split3(v)
    return dot(hi, onehot) + dot(mid, onehot) + dot(low, onehot)


def dot_exact_left(onehot, v):
    hi, mid, low = split3(v)
    return dot(onehot, hi) + dot(onehot, mid) + dot(onehot, low)


def silu(v):
    return v * (1.0 / (1.0 + jnp.exp(-v)))


def spread(rows, lanes, width):
    head = lax.broadcasted_iota(jnp.int32, (rows, lanes), 0)
    lane = lax.broadcasted_iota(jnp.int32, (rows, lanes), 1)
    return ((lane >= head * width) & (lane < head * width + width)).astype(F32).astype(BF16)


def conv_rolled(v, k):
    total = k[3:4] * v
    for shift in (1, 2, 3):
        total = total + k[3 - shift : 4 - shift] * pltpu.roll(v, shift, 0)
    return silu(total)


def conv_head(halo, v, k):
    joined = jnp.concatenate([halo[8:16].astype(F32), v[0:16].astype(F32)], axis=0)
    return conv_rolled(joined, k)[8:24]


def kernel(
    x_hbm, z_hbm, b_ref, c_ref, step_t, decay_t, kx_ref, kb_ref, kc_ref, skip_ref, gain_ref,
    w_hbm, o_ref,
    x_v, z_v, w_v, xc, bc, cc, halo_x, halo_b, halo_c,
    cum_t, cum_wide, in_w, gate_a, gate_b, scores, skip_wide,
    dl_send, dl_recv, dlx_send, dlx_recv,
    st_send, st_recv, excl, g_send, g_recv, pf_send, pf_recv, normed,
    diag_send, diag_recv, near_send, near_keep, near_recv, own,
    local_sem, halo_ssem, halo_rsem, dl_ssem, dl_rsem, dlx_ssem, dlx_rsem,
    st_ssem, st_rsem, g_ssem, g_rsem, pf_ssem, pf_rsem,
    diag_ssem, diag_rsem, near_ssem, near_rsem,
):
    ctx = lax.axis_index("ctx")
    y = lax.axis_index("head")
    ctx_count = LINE * XS
    xi = ctx // LINE
    pos = lax.rem(ctx, LINE)
    base = xi * LINE
    right = lax.rem(y + 1, 4)
    left = lax.rem(y + 3, 4)
    across = lax.rem(y + 2, 4)

    barrier = pltpu.get_barrier_semaphore()

    def greet_line(i, carry):
        pl.semaphore_signal(
            barrier, inc=1, device_id={"ctx": base + lax.rem(pos + i, LINE)}, device_id_type=MESH
        )
        return carry

    def greet_x(i, carry):
        pl.semaphore_signal(
            barrier, inc=1, device_id={"ctx": lax.rem(xi + i, XS) * LINE + pos}, device_id_type=MESH
        )
        return carry

    lax.fori_loop(1, LINE, greet_line, 0)
    lax.fori_loop(1, XS, greet_x, 0)
    for near in (right, left):
        pl.semaphore_signal(barrier, inc=1, device_id={"head": near}, device_id_type=MESH)
    for step in (1, ctx_count - 1):
        pl.semaphore_signal(
            barrier, inc=1, device_id={"ctx": lax.rem(ctx + step, ctx_count)}, device_id_type=MESH
        )

    load_x = pltpu.make_async_copy(x_hbm, x_v, local_sem.at[0])
    load_z = pltpu.make_async_copy(z_hbm, z_v, local_sem.at[1])
    load_w = pltpu.make_async_copy(w_hbm, w_v, local_sem.at[2])
    load_x.start()
    load_z.start()
    load_w.start()

    row = lax.broadcasted_iota(jnp.int32, (TOK, TOK), 0)
    col = lax.broadcasted_iota(jnp.int32, (TOK, TOK), 1)
    upper = (row <= col).astype(F32).astype(BF16)
    sums = dot_exact_right(decay_t[...], upper)
    cum_t[...] = sums
    cum = sums.T
    last = cum[TOK - 1 : TOK, :]
    weight = (jnp.exp(sums[:, TOK - 1 : TOK] - sums) * step_t[...]).T
    wide = spread(HEADS, HEADS * 128, 128)
    expand = spread(HEADS, CH, 64)
    cum_wide[...] = dot_exact_right(cum, wide)
    in_w[...] = dot_exact_right(weight, expand)
    dl_send[...] = dot_exact_right(jnp.broadcast_to(last, (8, HEADS)), spread(HEADS, N, 1))[0:1]

    load_x.wait()

    def conv_block(p, carry):
        lanes = pl.ds(pl.multiple_of(p * 128, 128), 128)
        xc[:, lanes] = conv_rolled(x_v[:, lanes].astype(F32), kx_ref[:, lanes].astype(F32)).astype(BF16)
        return carry

    lax.fori_loop(0, EARLY, conv_block, 0)

    pl.semaphore_wait(barrier, LINE - 1 + XS - 1 + 2 + 2)

    def halo_copies():
        parts = ((x_v, halo_x), (b_ref, halo_b), (c_ref, halo_c))
        return [
            pltpu.make_async_remote_copy(
                src_ref=src.at[pl.ds(TOK - 16, 16)],
                dst_ref=dst,
                send_sem=halo_ssem.at[i],
                recv_sem=halo_rsem.at[i],
                device_id={"ctx": lax.rem(ctx + 1, ctx_count)},
                device_id_type=MESH,
            )
            for i, (src, dst) in enumerate(parts)
        ]

    for copy in halo_copies():
        copy.start()

    def dl_copy(i, slot):
        to = lax.rem(pos + i, LINE)
        return pltpu.make_async_remote_copy(
            src_ref=dl_send,
            dst_ref=dl_recv.at[slot],
            send_sem=dl_ssem.at[i],
            recv_sem=dl_rsem.at[slot],
            device_id={"ctx": base + to},
            device_id_type=MESH,
        )

    def st_copy(i, slot):
        to = lax.rem(pos + i, LINE)
        return pltpu.make_async_remote_copy(
            src_ref=st_send.at[to],
            dst_ref=st_recv.at[slot],
            send_sem=st_ssem.at[i],
            recv_sem=st_rsem.at[slot],
            device_id={"ctx": base + to},
            device_id_type=MESH,
        )

    def pf_copy(i, slot):
        to = lax.rem(pos + i, LINE)
        return pltpu.make_async_remote_copy(
            src_ref=pf_send.at[to],
            dst_ref=pf_recv.at[slot],
            send_sem=pf_ssem.at[i],
            recv_sem=pf_rsem.at[slot],
            device_id={"ctx": base + to},
            device_id_type=MESH,
        )

    def dlx_copy(i, slot):
        return pltpu.make_async_remote_copy(
            src_ref=dlx_send,
            dst_ref=dlx_recv.at[slot],
            send_sem=dlx_ssem.at[i],
            recv_sem=dlx_rsem.at[slot],
            device_id={"ctx": lax.rem(xi + i, XS) * LINE + pos},
            device_id_type=MESH,
        )

    def g_copy(i, slot):
        return pltpu.make_async_remote_copy(
            src_ref=g_send,
            dst_ref=g_recv.at[slot],
            send_sem=g_ssem.at[i],
            recv_sem=g_rsem.at[slot],
            device_id={"ctx": lax.rem(xi + i, XS) * LINE + pos},
            device_id_type=MESH,
        )

    def start_later(make):
        for i in range(1, XS):
            @pl.when(xi + i < XS)
            def _(i=i):
                make(i, xi).start()

    def wait_earlier(make):
        for i in range(1, XS):
            @pl.when(xi + i < XS)
            def _(i=i):
                make(i, xi).wait_send()

            @pl.when(xi >= i)
            def _(i=i):
                make(i, xi - i).wait_recv()

    def start_all(make, count, here):
        def one(i, carry):
            make(i, here).start()
            return carry

        lax.fori_loop(1, count, one, 0)

    def wait_all(make, count, here):
        def one(i, carry):
            copy = make(i, lax.rem(here + i, count))
            copy.wait_send()
            copy.wait_recv()
            return carry

        lax.fori_loop(1, count, one, 0)

    start_all(dl_copy, LINE, pos)

    lax.fori_loop(EARLY, CH // 128, conv_block, 0)
    bc[...] = conv_rolled(b_ref[...].astype(F32), kb_ref[...].astype(F32)).astype(BF16)
    cc[...] = conv_rolled(c_ref[...].astype(F32), kc_ref[...].astype(F32)).astype(BF16)

    for copy in halo_copies():
        copy.wait()

    first = ctx == 0

    def halo_value(ref):
        v = ref[...].astype(F32)
        return jnp.where(first, jnp.zeros_like(v), v)

    xc[0:16, :] = conv_head(halo_value(halo_x), x_v[0:16, :], kx_ref[...].astype(F32)).astype(BF16)
    bc[0:16, :] = conv_head(halo_value(halo_b), b_ref[0:16, :], kb_ref[...].astype(F32)).astype(BF16)
    cc[0:16, :] = conv_head(halo_value(halo_c), c_ref[0:16, :], kc_ref[...].astype(F32)).astype(BF16)

    b_cols = bc[...].astype(F32).T.astype(BF16)

    def state_block(p, carry):
        lanes = pl.ds(pl.multiple_of(p * 128, 128), 128)
        scaled = (xc[:, lanes].astype(F32) * in_w[:, lanes]).astype(BF16)
        st_send[:, :, lanes] = dot(b_cols, scaled).reshape(LINE, ROWS, 128).astype(BF16)
        return carry

    lax.fori_loop(0, CH // 128, state_block, 0)
    st_recv[pos] = st_send[pos]
    start_all(st_copy, LINE, pos)

    dl_recv[pos] = dl_send[...]
    wait_all(dl_copy, LINE, pos)
    line_decay = dl_recv[:, 0, :]
    dlx_send[...] = jnp.sum(line_decay, axis=0, keepdims=True)
    dlx_recv[xi] = dlx_send[...]
    start_all(dlx_copy, XS, xi)

    scores[...] = dot(cc[...], b_cols)
    in_w[...] = dot_exact_right(jnp.exp(cum), expand)
    skip_row = dot_exact_right(jnp.broadcast_to(skip_ref[...], (8, HEADS)), expand)[0:1]
    skip_wide[...] = skip_row
    load_z.wait()
    trow = lax.broadcasted_iota(jnp.int32, (128, 128), 0)
    tcol = lax.broadcasted_iota(jnp.int32, (128, 128), 1)
    causal = trow >= tcol

    def span_block(p, carry):
        lanes = pl.ds(pl.multiple_of(p * 128, 128), 128)
        x_pair = xc[:, lanes]
        tops, bottoms = [], []
        for e in range(2):
            h = 2 * p + e
            cols = cum_wide[:, pl.ds(pl.multiple_of(h * 128, 128), 128)]
            cum_row = cum_t[pl.ds(h, 1), :]
            step_row = step_t[pl.ds(h, 1), :]

            def mix(t, s, masked):
                gap = cols[t : t + 128] - cum_row[:, s : s + 128]
                if masked:
                    gap = jnp.where(causal, gap, -1e30)
                m = scores[t : t + 128, s : s + 128] * jnp.exp(gap) * step_row[:, s : s + 128]
                return m.astype(BF16)

            tops.append(dot(mix(0, 0, True), x_pair[0:128]))
            bottoms.append(
                dot(mix(128, 0, False), x_pair[0:128]) + dot(mix(128, 128, True), x_pair[128:256])
            )
        low = tcol < 64
        inner = jnp.concatenate(
            [jnp.where(low, tops[0], tops[1]), jnp.where(low, bottoms[0], bottoms[1])], axis=0
        )
        gate = silu(z_v[:, lanes].astype(F32))
        gate_a[:, lanes] = (inner + skip_wide[:, lanes] * x_pair.astype(F32)) * gate
        gate_b[:, lanes] = in_w[:, lanes] * gate
        return carry

    lax.fori_loop(0, CH // 128, span_block, 0)

    expand_n = spread(N, CH, 64)
    line_factor = jnp.exp(dot_exact_right(line_decay, expand_n))
    wait_all(st_copy, LINE, pos)
    running = jnp.zeros((ROWS, CH), F32)
    for j in range(LINE):
        excl[j] = running
        running = line_factor[j : j + 1] * running + st_recv[j].astype(F32)
    g_send[...] = running
    start_later(g_copy)

    wait_all(dlx_copy, XS, xi)
    x_decay = dlx_recv[:, 0, :]
    x_factor = jnp.exp(
        dot_exact_right(jnp.concatenate([x_decay, x_decay], axis=0), expand_n)
    )
    wait_earlier(g_copy)
    before = jnp.zeros((ROWS, CH), F32)
    for i in range(XS - 1):
        before = jnp.where(i < xi, x_factor[i : i + 1] * before + g_recv[i], before)
    for j in range(LINE):
        pf_send[j] = (excl[j] + before).astype(BF16)
        before = line_factor[j : j + 1] * before
    pf_recv[pos] = pf_send[pos]
    start_all(pf_copy, LINE, pos)
    wait_all(pf_copy, LINE, pos)

    state = pf_recv[...].astype(F32).reshape(N, CH).astype(BF16)
    c_all = cc[...]
    squares = jnp.zeros((TOK, 128), F32)
    for p in range(CH // 256):
        lanes = slice(p * 256, p * 256 + 256)
        gated = gate_a[:, lanes] + dot(c_all, state[:, lanes]) * gate_b[:, lanes]
        gate_a[:, lanes] = gated
        sq = gated * gated
        squares = squares + sq[:, 0:128] + sq[:, 128:256]
    scale = lax.rsqrt(jnp.sum(squares, axis=1, keepdims=True) * (1.0 / CH) + 1e-05)
    for p in range(CH // 256):
        lanes = slice(p * 256, p * 256 + 256)
        normed[:, lanes] = (gate_a[:, lanes] * scale * gain_ref[:, lanes]).astype(BF16)

    load_w.wait()

    def product(owner, j):
        lanes = pl.ds(pl.multiple_of(owner * CH + j * PW, PW), PW)
        return dot(normed[...], w_v[:, lanes])

    sides = (right, left)
    diag_rows = (0, 128)
    near_rows = (128, 0)

    def diag_copy(side, j):
        return pltpu.make_async_remote_copy(
            src_ref=diag_send.at[side, j],
            dst_ref=diag_recv.at[side, j],
            send_sem=diag_ssem.at[side, j],
            recv_sem=diag_rsem.at[side, j],
            device_id={"head": sides[side]},
            device_id_type=MESH,
        )

    def near_copy(side, relayed, j):
        return pltpu.make_async_remote_copy(
            src_ref=near_send.at[side, relayed, j],
            dst_ref=near_recv.at[side, relayed, j],
            send_sem=near_ssem.at[side, relayed, j],
            recv_sem=near_rsem.at[side, relayed, j],
            device_id={"head": sides[side]},
            device_id_type=MESH,
        )

    def across_step(j, carry):
        part = product(across, j).astype(BF16)
        for side in range(2):
            diag_send[side, j] = part[diag_rows[side] : diag_rows[side] + 128]
            diag_copy(side, j).start()
        return carry

    lax.fori_loop(0, PIECES, across_step, 0)

    def near_step(j, carry):
        for side in range(2):
            part = product(sides[side], j).astype(BF16)
            near_send[side, 0, j] = part[near_rows[side] : near_rows[side] + 128]
            near_copy(side, 0, j).start()
            near_keep[side, j] = part[diag_rows[side] : diag_rows[side] + 128]
        return carry

    lax.fori_loop(0, PIECES, near_step, 0)

    def relay_step(j, carry):
        for side in range(2):
            diag_copy(side, j).wait()
            total = near_keep[side, j].astype(F32) + diag_recv[side, j].astype(F32)
            near_send[side, 1, j] = total.astype(BF16)
            near_copy(side, 1, j).start()
        return carry

    lax.fori_loop(0, PIECES, relay_step, 0)

    def own_step(j, carry):
        own[j] = product(y, j)
        return carry

    lax.fori_loop(0, PIECES, own_step, 0)

    for relayed in range(2):
        def last_step(j, carry):
            for side in range(2):
                near_copy(side, relayed, j).wait()
            return carry

        lax.fori_loop(0, PIECES, last_step, 0)
    for j in range(PIECES):
        lanes = slice(j * PW, j * PW + PW)
        mine = own[j].astype(BF16).astype(F32)
        top = near_recv[0, 1, j].astype(F32) + near_recv[1, 0, j].astype(F32)
        bottom = near_recv[0, 0, j].astype(F32) + near_recv[1, 1, j].astype(F32)
        o_ref[0:128, lanes] = (mine[0:128] + top).astype(BF16)
        o_ref[128:256, lanes] = (mine[128:256] + bottom).astype(BF16)


def body(x, z, b, c, step, decay, kx, kb, kc, skip, gain, w):
    vm = pl.BlockSpec(memory_space=pltpu.VMEM)
    hbm = pl.BlockSpec(memory_space=pl.ANY)
    dma = pltpu.SemaphoreType.DMA
    return pl.pallas_call(
        kernel,
        out_shape=jax.ShapeDtypeStruct((TOK, CH), BF16),
        in_specs=[hbm, hbm] + [vm] * 9 + [hbm],
        out_specs=vm,
        scratch_shapes=[
            pltpu.VMEM((TOK, CH), BF16),
            pltpu.VMEM((TOK, CH), BF16),
            pltpu.VMEM((CH, 4 * CH), BF16),
            pltpu.VMEM((TOK, CH), BF16),
            pltpu.VMEM((TOK, N), BF16),
            pltpu.VMEM((TOK, N), BF16),
            pltpu.VMEM((16, CH), BF16),
            pltpu.VMEM((16, N), BF16),
            pltpu.VMEM((16, N), BF16),
            pltpu.VMEM((HEADS, TOK), F32),
            pltpu.VMEM((TOK, HEADS * 128), F32),
            pltpu.VMEM((TOK, CH), F32),
            pltpu.VMEM((TOK, CH), F32),
            pltpu.VMEM((TOK, CH), F32),
            pltpu.VMEM((TOK, TOK), F32),
            pltpu.VMEM((1, CH), F32),
            pltpu.VMEM((1, N), F32),
            pltpu.VMEM((LINE, 1, N), F32),
            pltpu.VMEM((1, N), F32),
            pltpu.VMEM((XS, 1, N), F32),
            pltpu.VMEM((LINE, ROWS, CH), BF16),
            pltpu.VMEM((LINE, ROWS, CH), BF16),
            pltpu.VMEM((LINE, ROWS, CH), F32),
            pltpu.VMEM((ROWS, CH), F32),
            pltpu.VMEM((XS, ROWS, CH), F32),
            pltpu.VMEM((LINE, ROWS, CH), BF16),
            pltpu.VMEM((LINE, ROWS, CH), BF16),
            pltpu.VMEM((TOK, CH), BF16),
            pltpu.VMEM((2, PIECES, 128, PW), BF16),
            pltpu.VMEM((2, PIECES, 128, PW), BF16),
            pltpu.VMEM((2, 2, PIECES, 128, PW), BF16),
            pltpu.VMEM((2, PIECES, 128, PW), BF16),
            pltpu.VMEM((2, 2, PIECES, 128, PW), BF16),
            pltpu.VMEM((PIECES, TOK, PW), F32),
            dma((3,)),
            dma((3,)),
            dma((3,)),
            dma((LINE,)),
            dma((LINE,)),
            dma((XS,)),
            dma((XS,)),
            dma((LINE,)),
            dma((LINE,)),
            dma((XS,)),
            dma((XS,)),
            dma((LINE,)),
            dma((LINE,)),
            dma((2, PIECES)),
            dma((2, PIECES)),
            dma((2, 2, PIECES)),
            dma((2, 2, PIECES)),
        ],
        compiler_params=pltpu.CompilerParams(collective_id=0, has_side_effects=True),
        name="ssm_layer",
    )(x, z, b, c, step.T, decay.T, kx, kb, kc, skip.reshape(1, HEADS), gain.reshape(1, CH), w)


def solution(mesh):
    placed = (
        P("ctx", "head"),
        P("ctx", "head"),
        P("ctx", "head"),
        P("ctx", "head"),
        P("ctx", "head"),
        P("ctx", "head"),
        P(None, "head"),
        P(None, "head"),
        P(None, "head"),
        P("head"),
        P("head"),
        P("head", None),
    )
    return jax.shard_map(
        body, mesh=mesh, in_specs=placed, out_specs=P("ctx", "head"), check_vma=False
    )
```

```python
import jax
import jax.numpy as jnp
from jax import lax
from jax.experimental import pallas as pl
from jax.experimental.pallas import tpu as pltpu
from jax.sharding import PartitionSpec as P

TOK = 256
CH = 1024
HEADS = 16
N = 128
LINE = 16
XS = 4
ROWS = N // LINE
PIECES = 4
PW = CH // PIECES
MESH = pl.DeviceIdType.MESH
F32 = jnp.float32
BF16 = jnp.bfloat16


def dot(a, b):
    return jnp.dot(a, b, preferred_element_type=F32)


def split3(v):
    hi = v.astype(BF16)
    rest = v - hi.astype(F32)
    mid = rest.astype(BF16)
    low = (rest - mid.astype(F32)).astype(BF16)
    return hi, mid, low


def dot_exact_right(v, onehot):
    hi, mid, low = split3(v)
    return dot(hi, onehot) + dot(mid, onehot) + dot(low, onehot)


def dot_exact_left(onehot, v):
    hi, mid, low = split3(v)
    return dot(onehot, hi) + dot(onehot, mid) + dot(onehot, low)


def silu(v):
    return v * (1.0 / (1.0 + jnp.exp(-v)))


def spread(rows, lanes, width):
    head = lax.broadcasted_iota(jnp.int32, (rows, lanes), 0)
    lane = lax.broadcasted_iota(jnp.int32, (rows, lanes), 1)
    return ((lane >= head * width) & (lane < head * width + width)).astype(F32).astype(BF16)


def conv_rolled(v, k):
    total = k[3:4] * v
    for shift in (1, 2, 3):
        total = total + k[3 - shift : 4 - shift] * pltpu.roll(v, shift, 0)
    return silu(total)


def conv_head(halo, v, k):
    joined = jnp.concatenate([halo[8:16].astype(F32), v[0:16].astype(F32)], axis=0)
    return conv_rolled(joined, k)[8:24]


def kernel(
    x_hbm, z_hbm, b_ref, c_ref, step_t, decay_t, kx_ref, kb_ref, kc_ref, skip_ref, gain_ref,
    w_hbm, o_ref,
    x_v, z_v, w_v, xc, bc, cc, halo_x, halo_b, halo_c,
    cum_t, cum_wide, in_w, gate_a, gate_b, scores, skip_wide,
    dl_send, dl_recv, dlx_send, dlx_recv,
    st_send, st_recv, excl, g_send, g_recv, pf_send, pf_recv, normed,
    diag_send, diag_recv, near_send, near_keep, near_recv, own,
    local_sem, halo_ssem, halo_rsem, dl_ssem, dl_rsem, dlx_ssem, dlx_rsem,
    st_ssem, st_rsem, g_ssem, g_rsem, pf_ssem, pf_rsem,
    diag_ssem, diag_rsem, near_ssem, near_rsem,
):
    ctx = lax.axis_index("ctx")
    y = lax.axis_index("head")
    ctx_count = LINE * XS
    xi = ctx // LINE
    pos = lax.rem(ctx, LINE)
    base = xi * LINE
    right = lax.rem(y + 1, 4)
    left = lax.rem(y + 3, 4)
    across = lax.rem(y + 2, 4)

    barrier = pltpu.get_barrier_semaphore()

    def greet_line(i, carry):
        pl.semaphore_signal(
            barrier, inc=1, device_id={"ctx": base + lax.rem(pos + i, LINE)}, device_id_type=MESH
        )
        return carry

    def greet_x(i, carry):
        pl.semaphore_signal(
            barrier, inc=1, device_id={"ctx": lax.rem(xi + i, XS) * LINE + pos}, device_id_type=MESH
        )
        return carry

    lax.fori_loop(1, LINE, greet_line, 0)
    lax.fori_loop(1, XS, greet_x, 0)
    for near in (right, left):
        pl.semaphore_signal(barrier, inc=1, device_id={"head": near}, device_id_type=MESH)
    for step in (1, ctx_count - 1):
        pl.semaphore_signal(
            barrier, inc=1, device_id={"ctx": lax.rem(ctx + step, ctx_count)}, device_id_type=MESH
        )

    load_x = pltpu.make_async_copy(x_hbm, x_v, local_sem.at[0])
    load_z = pltpu.make_async_copy(z_hbm, z_v, local_sem.at[1])
    load_w = pltpu.make_async_copy(w_hbm, w_v, local_sem.at[2])
    load_x.start()
    load_z.start()
    load_w.start()

    row = lax.broadcasted_iota(jnp.int32, (TOK, TOK), 0)
    col = lax.broadcasted_iota(jnp.int32, (TOK, TOK), 1)
    upper = (row <= col).astype(F32).astype(BF16)
    sums = dot_exact_right(decay_t[...], upper)
    cum_t[...] = sums
    cum = sums.T
    last = cum[TOK - 1 : TOK, :]
    weight = (jnp.exp(sums[:, TOK - 1 : TOK] - sums) * step_t[...]).T
    wide = spread(HEADS, HEADS * 128, 128)
    expand = spread(HEADS, CH, 64)
    cum_wide[...] = dot_exact_right(cum, wide)
    in_w[...] = dot_exact_right(weight, expand)
    dl_send[...] = dot_exact_right(jnp.broadcast_to(last, (8, HEADS)), spread(HEADS, N, 1))[0:1]

    load_x.wait()

    def conv_block(p, carry):
        lanes = pl.ds(pl.multiple_of(p * 128, 128), 128)
        xc[:, lanes] = conv_rolled(x_v[:, lanes].astype(F32), kx_ref[:, lanes].astype(F32)).astype(BF16)
        return carry

    lax.fori_loop(0, CH // 128, conv_block, 0)
    bc[...] = conv_rolled(b_ref[...].astype(F32), kb_ref[...].astype(F32)).astype(BF16)
    cc[...] = conv_rolled(c_ref[...].astype(F32), kc_ref[...].astype(F32)).astype(BF16)

    pl.semaphore_wait(barrier, LINE - 1 + XS - 1 + 2 + 2)

    def halo_copies():
        parts = ((x_v, halo_x), (b_ref, halo_b), (c_ref, halo_c))
        return [
            pltpu.make_async_remote_copy(
                src_ref=src.at[pl.ds(TOK - 16, 16)],
                dst_ref=dst,
                send_sem=halo_ssem.at[i],
                recv_sem=halo_rsem.at[i],
                device_id={"ctx": lax.rem(ctx + 1, ctx_count)},
                device_id_type=MESH,
            )
            for i, (src, dst) in enumerate(parts)
        ]

    for copy in halo_copies():
        copy.start()

    def dl_copy(i, slot):
        to = lax.rem(pos + i, LINE)
        return pltpu.make_async_remote_copy(
            src_ref=dl_send,
            dst_ref=dl_recv.at[slot],
            send_sem=dl_ssem.at[i],
            recv_sem=dl_rsem.at[slot],
            device_id={"ctx": base + to},
            device_id_type=MESH,
        )

    def st_copy(i, slot):
        to = lax.rem(pos + i, LINE)
        return pltpu.make_async_remote_copy(
            src_ref=st_send.at[to],
            dst_ref=st_recv.at[slot],
            send_sem=st_ssem.at[i],
            recv_sem=st_rsem.at[slot],
            device_id={"ctx": base + to},
            device_id_type=MESH,
        )

    def pf_copy(i, slot):
        to = lax.rem(pos + i, LINE)
        return pltpu.make_async_remote_copy(
            src_ref=pf_send.at[to],
            dst_ref=pf_recv.at[slot],
            send_sem=pf_ssem.at[i],
            recv_sem=pf_rsem.at[slot],
            device_id={"ctx": base + to},
            device_id_type=MESH,
        )

    def dlx_copy(i, slot):
        return pltpu.make_async_remote_copy(
            src_ref=dlx_send,
            dst_ref=dlx_recv.at[slot],
            send_sem=dlx_ssem.at[i],
            recv_sem=dlx_rsem.at[slot],
            device_id={"ctx": lax.rem(xi + i, XS) * LINE + pos},
            device_id_type=MESH,
        )

    def g_copy(i, slot):
        return pltpu.make_async_remote_copy(
            src_ref=g_send,
            dst_ref=g_recv.at[slot],
            send_sem=g_ssem.at[i],
            recv_sem=g_rsem.at[slot],
            device_id={"ctx": lax.rem(xi + i, XS) * LINE + pos},
            device_id_type=MESH,
        )

    def start_later(make):
        for i in range(1, XS):
            @pl.when(xi + i < XS)
            def _(i=i):
                make(i, xi).start()

    def wait_earlier(make):
        for i in range(1, XS):
            @pl.when(xi + i < XS)
            def _(i=i):
                make(i, xi).wait_send()

            @pl.when(xi >= i)
            def _(i=i):
                make(i, xi - i).wait_recv()

    def start_all(make, count, here):
        def one(i, carry):
            make(i, here).start()
            return carry

        lax.fori_loop(1, count, one, 0)

    def wait_all(make, count, here):
        def one(i, carry):
            copy = make(i, lax.rem(here + i, count))
            copy.wait_send()
            copy.wait_recv()
            return carry

        lax.fori_loop(1, count, one, 0)

    start_all(dl_copy, LINE, pos)

    for copy in halo_copies():
        copy.wait()

    first = ctx == 0

    def halo_value(ref):
        v = ref[...].astype(F32)
        return jnp.where(first, jnp.zeros_like(v), v)

    xc[0:16, :] = conv_head(halo_value(halo_x), x_v[0:16, :], kx_ref[...].astype(F32)).astype(BF16)
    bc[0:16, :] = conv_head(halo_value(halo_b), b_ref[0:16, :], kb_ref[...].astype(F32)).astype(BF16)
    cc[0:16, :] = conv_head(halo_value(halo_c), c_ref[0:16, :], kc_ref[...].astype(F32)).astype(BF16)

    b_cols = bc[...].astype(F32).T.astype(BF16)

    def state_block(p, carry):
        lanes = pl.ds(pl.multiple_of(p * 128, 128), 128)
        scaled = (xc[:, lanes].astype(F32) * in_w[:, lanes]).astype(BF16)
        st_send[:, :, lanes] = dot(b_cols, scaled).reshape(LINE, ROWS, 128).astype(BF16)
        return carry

    lax.fori_loop(0, CH // 128, state_block, 0)
    st_recv[pos] = st_send[pos]
    start_all(st_copy, LINE, pos)

    dl_recv[pos] = dl_send[...]
    wait_all(dl_copy, LINE, pos)
    line_decay = dl_recv[:, 0, :]
    dlx_send[...] = jnp.sum(line_decay, axis=0, keepdims=True)
    dlx_recv[xi] = dlx_send[...]
    start_all(dlx_copy, XS, xi)

    scores[...] = dot(cc[...], b_cols)
    in_w[...] = dot_exact_right(jnp.exp(cum), expand)
    skip_row = dot_exact_right(jnp.broadcast_to(skip_ref[...], (8, HEADS)), expand)[0:1]
    skip_wide[...] = skip_row
    load_z.wait()
    trow = lax.broadcasted_iota(jnp.int32, (128, 128), 0)
    tcol = lax.broadcasted_iota(jnp.int32, (128, 128), 1)
    causal = trow >= tcol

    def span_block(p, carry):
        lanes = pl.ds(pl.multiple_of(p * 128, 128), 128)
        x_pair = xc[:, lanes]
        tops, bottoms = [], []
        for e in range(2):
            h = 2 * p + e
            cols = cum_wide[:, pl.ds(pl.multiple_of(h * 128, 128), 128)]
            cum_row = cum_t[pl.ds(h, 1), :]
            step_row = step_t[pl.ds(h, 1), :]

            def mix(t, s, masked):
                gap = cols[t : t + 128] - cum_row[:, s : s + 128]
                if masked:
                    gap = jnp.where(causal, gap, -1e30)
                m = scores[t : t + 128, s : s + 128] * jnp.exp(gap) * step_row[:, s : s + 128]
                return m.astype(BF16)

            tops.append(dot(mix(0, 0, True), x_pair[0:128]))
            bottoms.append(
                dot(mix(128, 0, False), x_pair[0:128]) + dot(mix(128, 128, True), x_pair[128:256])
            )
        low = tcol < 64
        inner = jnp.concatenate(
            [jnp.where(low, tops[0], tops[1]), jnp.where(low, bottoms[0], bottoms[1])], axis=0
        )
        gate = silu(z_v[:, lanes].astype(F32))
        gate_a[:, lanes] = (inner + skip_wide[:, lanes] * x_pair.astype(F32)) * gate
        gate_b[:, lanes] = in_w[:, lanes] * gate
        return carry

    lax.fori_loop(0, CH // 128, span_block, 0)

    expand_n = spread(N, CH, 64)
    line_factor = jnp.exp(dot_exact_right(line_decay, expand_n))
    running = jnp.zeros((ROWS, CH), F32)
    for j in range(LINE):
        excl[j] = running

        @pl.when(pos != j)
        def _(j=j):
            copy = st_copy(lax.rem(j - pos + LINE, LINE), j)
            copy.wait_send()
            copy.wait_recv()

        running = line_factor[j : j + 1] * running + st_recv[j].astype(F32)
    g_send[...] = running
    start_later(g_copy)

    wait_all(dlx_copy, XS, xi)
    x_decay = dlx_recv[:, 0, :]
    x_factor = jnp.exp(
        dot_exact_right(jnp.concatenate([x_decay, x_decay], axis=0), expand_n)
    )
    wait_earlier(g_copy)
    def start_prefix(j):
        @pl.when(pos != j)
        def _():
            pf_copy(lax.rem(j - pos + LINE, LINE), pos).start()

    before = jnp.zeros((ROWS, CH), F32)
    for i in range(XS - 1):
        before = jnp.where(i < xi, x_factor[i : i + 1] * before + g_recv[i], before)
    for j in range(LINE):
        pf_send[j] = (excl[j] + before).astype(BF16)
        before = line_factor[j : j + 1] * before
        if j > 0:
            start_prefix(j - 1)
    pf_recv[pos] = pf_send[pos]
    start_prefix(LINE - 1)
    wait_all(pf_copy, LINE, pos)

    state = pf_recv[...].astype(F32).reshape(N, CH).astype(BF16)
    c_all = cc[...]
    squares = jnp.zeros((TOK, 128), F32)
    for p in range(CH // 256):
        lanes = slice(p * 256, p * 256 + 256)
        gated = gate_a[:, lanes] + dot(c_all, state[:, lanes]) * gate_b[:, lanes]
        gate_a[:, lanes] = gated
        sq = gated * gated
        squares = squares + sq[:, 0:128] + sq[:, 128:256]
    scale = lax.rsqrt(jnp.sum(squares, axis=1, keepdims=True) * (1.0 / CH) + 1e-05)
    for p in range(CH // 256):
        lanes = slice(p * 256, p * 256 + 256)
        normed[:, lanes] = (gate_a[:, lanes] * scale * gain_ref[:, lanes]).astype(BF16)

    load_w.wait()

    def product(owner, j):
        lanes = pl.ds(pl.multiple_of(owner * CH + j * PW, PW), PW)
        return dot(normed[...], w_v[:, lanes])

    sides = (right, left)
    diag_rows = (0, 128)
    near_rows = (128, 0)

    def diag_copy(side, j):
        return pltpu.make_async_remote_copy(
            src_ref=diag_send.at[side, j],
            dst_ref=diag_recv.at[side, j],
            send_sem=diag_ssem.at[side, j],
            recv_sem=diag_rsem.at[side, j],
            device_id={"head": sides[side]},
            device_id_type=MESH,
        )

    def near_copy(side, relayed, j):
        return pltpu.make_async_remote_copy(
            src_ref=near_send.at[side, relayed, j],
            dst_ref=near_recv.at[side, relayed, j],
            send_sem=near_ssem.at[side, relayed, j],
            recv_sem=near_rsem.at[side, relayed, j],
            device_id={"head": sides[side]},
            device_id_type=MESH,
        )

    def across_step(j, carry):
        part = product(across, j).astype(BF16)
        for side in range(2):
            diag_send[side, j] = part[diag_rows[side] : diag_rows[side] + 128]
            diag_copy(side, j).start()
        return carry

    lax.fori_loop(0, PIECES, across_step, 0)

    def near_step(j, carry):
        for side in range(2):
            part = product(sides[side], j).astype(BF16)
            near_send[side, 0, j] = part[near_rows[side] : near_rows[side] + 128]
            near_copy(side, 0, j).start()
            near_keep[side, j] = part[diag_rows[side] : diag_rows[side] + 128]
        return carry

    lax.fori_loop(0, PIECES, near_step, 0)

    def relay_step(j, carry):
        for side in range(2):
            diag_copy(side, j).wait()
            total = near_keep[side, j].astype(F32) + diag_recv[side, j].astype(F32)
            near_send[side, 1, j] = total.astype(BF16)
            near_copy(side, 1, j).start()
        return carry

    lax.fori_loop(0, PIECES, relay_step, 0)

    def own_step(j, carry):
        own[j] = product(y, j)
        return carry

    lax.fori_loop(0, PIECES, own_step, 0)

    def first_step(j, carry):
        for side in range(2):
            near_copy(side, 0, j).wait()
        return carry

    lax.fori_loop(0, PIECES, first_step, 0)
    for j in range(PIECES):
        for side in range(2):
            near_copy(side, 1, j).wait()
        lanes = slice(j * PW, j * PW + PW)
        mine = own[j].astype(BF16).astype(F32)
        top = near_recv[0, 1, j].astype(F32) + near_recv[1, 0, j].astype(F32)
        bottom = near_recv[0, 0, j].astype(F32) + near_recv[1, 1, j].astype(F32)
        o_ref[0:128, lanes] = (mine[0:128] + top).astype(BF16)
        o_ref[128:256, lanes] = (mine[128:256] + bottom).astype(BF16)


def body(x, z, b, c, step, decay, kx, kb, kc, skip, gain, w):
    vm = pl.BlockSpec(memory_space=pltpu.VMEM)
    hbm = pl.BlockSpec(memory_space=pl.ANY)
    dma = pltpu.SemaphoreType.DMA
    return pl.pallas_call(
        kernel,
        out_shape=jax.ShapeDtypeStruct((TOK, CH), BF16),
        in_specs=[hbm, hbm] + [vm] * 9 + [hbm],
        out_specs=vm,
        scratch_shapes=[
            pltpu.VMEM((TOK, CH), BF16),
            pltpu.VMEM((TOK, CH), BF16),
            pltpu.VMEM((CH, 4 * CH), BF16),
            pltpu.VMEM((TOK, CH), BF16),
            pltpu.VMEM((TOK, N), BF16),
            pltpu.VMEM((TOK, N), BF16),
            pltpu.VMEM((16, CH), BF16),
            pltpu.VMEM((16, N), BF16),
            pltpu.VMEM((16, N), BF16),
            pltpu.VMEM((HEADS, TOK), F32),
            pltpu.VMEM((TOK, HEADS * 128), F32),
            pltpu.VMEM((TOK, CH), F32),
            pltpu.VMEM((TOK, CH), F32),
            pltpu.VMEM((TOK, CH), F32),
            pltpu.VMEM((TOK, TOK), F32),
            pltpu.VMEM((1, CH), F32),
            pltpu.VMEM((1, N), F32),
            pltpu.VMEM((LINE, 1, N), F32),
            pltpu.VMEM((1, N), F32),
            pltpu.VMEM((XS, 1, N), F32),
            pltpu.VMEM((LINE, ROWS, CH), BF16),
            pltpu.VMEM((LINE, ROWS, CH), BF16),
            pltpu.VMEM((LINE, ROWS, CH), F32),
            pltpu.VMEM((ROWS, CH), F32),
            pltpu.VMEM((XS, ROWS, CH), F32),
            pltpu.VMEM((LINE, ROWS, CH), BF16),
            pltpu.VMEM((LINE, ROWS, CH), BF16),
            pltpu.VMEM((TOK, CH), BF16),
            pltpu.VMEM((2, PIECES, 128, PW), BF16),
            pltpu.VMEM((2, PIECES, 128, PW), BF16),
            pltpu.VMEM((2, 2, PIECES, 128, PW), BF16),
            pltpu.VMEM((2, PIECES, 128, PW), BF16),
            pltpu.VMEM((2, 2, PIECES, 128, PW), BF16),
            pltpu.VMEM((PIECES, TOK, PW), F32),
            dma((3,)),
            dma((3,)),
            dma((3,)),
            dma((LINE,)),
            dma((LINE,)),
            dma((XS,)),
            dma((XS,)),
            dma((LINE,)),
            dma((LINE,)),
            dma((XS,)),
            dma((XS,)),
            dma((LINE,)),
            dma((LINE,)),
            dma((2, PIECES)),
            dma((2, PIECES)),
            dma((2, 2, PIECES)),
            dma((2, 2, PIECES)),
        ],
        compiler_params=pltpu.CompilerParams(collective_id=0, has_side_effects=True),
        name="ssm_layer",
    )(x, z, b, c, step.T, decay.T, kx, kb, kc, skip.reshape(1, HEADS), gain.reshape(1, CH), w)


def solution(mesh):
    placed = (
        P("ctx", "head"),
        P("ctx", "head"),
        P("ctx", "head"),
        P("ctx", "head"),
        P("ctx", "head"),
        P("ctx", "head"),
        P(None, "head"),
        P(None, "head"),
        P(None, "head"),
        P("head"),
        P("head"),
        P("head", None),
    )
    return jax.shard_map(
        body, mesh=mesh, in_specs=placed, out_specs=P("ctx", "head"), check_vma=False
    )
```
